32 devices in a mesh: copies: 2 (over y), blk: 4 (over x, core), virt: 4 (over z).
Axes of the slice: x: 2, y: 2, z: 4, core: 2. Of those that a mesh axis runs over, the one named last changes fastest.
Arguments:
- three_index: bfloat16 [32, 512, 2048], P(('copies', 'blk'), 'virt'), parts along dimension 0, may hold values from -0.59765625 to 0.59765625
- occ_energy: float32 [32], P(('copies', 'blk')), parts along dimension 0, may hold values from -2 to -0.5
- virt_energy: float32 [1024], P('copies'), parts along dimension 0, may hold values from 0.3 to 3
Outputs:
- gradient: bfloat16 [32, 512, 2048], P(('copies', 'blk'), 'virt'), parts along dimension 0
The draws below stay inside these ranges and needn't reach their ends.
There are 2 independent parts, one for each index of `copies`. The reference program is written for one: setup_inputs(seed, part) draws one part's arguments, and reference() takes and returns one part's arrays. A program takes and returns all parts, laid end to end along the dimension named above; each array names one. Nothing has to cross between parts.
All inputs are finite; a program needn't handle non-finite values.
Results may differ from the reference program's by a relative error of at most 0.0055.
Values may be sent and summed in bfloat16 or wider, within the bound.
A program may use at most 64 MiB of HBM per device.

```python
import jax
import jax.numpy as jnp
from jax import lax

OCC_BLK = 4
VIRT = 512
AUX = 2048
NOCC = 16
N_BLK = 4


def level_of(own_key, shape, cuts, smallest, largest):
    loudness = 1.0
    for position, parts in cuts:
        heights = jax.random.uniform(jax.random.fold_in(jax.random.fold_in(own_key, 6), position), (parts,), jnp.float32, smallest / len(cuts), largest / len(cuts))
        loudness = loudness * jnp.repeat(jnp.exp(heights), shape[position] // parts).reshape((-1,) + (1,) * (len(shape) - 1 - position))
    return loudness


def bell_draw(stream_key, dims, width, reach, cuts=(), kind=jnp.bfloat16):
    drawn = width * jax.random.normal(stream_key, dims, jnp.float32)
    if cuts:
        drawn = drawn * level_of(stream_key, dims, cuts, -0.22, 0.18)
    return jnp.clip(drawn, -reach, reach).astype(kind)


def setup_inputs(seed: int = 0, part: int = 0) -> dict:
    key_list = jax.random.split(jax.random.key(seed), 4)
    own_keys = jax.random.split(jax.random.fold_in(key_list[3], part), 4)
    return {
        "three_index": bell_draw(own_keys[0], (NOCC, VIRT, AUX), 0.1, 0.59765625, ((0, 4), (1, 4))),
        "occ_energy": jnp.clip(-2.0 + 1.5 * jax.random.uniform(own_keys[1], (NOCC,), jnp.float32) ** level_of(own_keys[1], (NOCC,), ((0, 4),), -0.2, 0.2), -2.0, -0.5),
        "virt_energy": jnp.clip(jax.random.uniform(own_keys[2], (VIRT,), jnp.float32, 0.3, 3.0), 0.3, 3.0),
    }


def pair_terms(block_own, block_part, energy_own, energy_part, virt_energy):
    occ_count, virt_count, aux_count = block_own.shape
    first = jnp.dot(block_own.reshape(occ_count * virt_count, aux_count), block_part.reshape(occ_count * virt_count, aux_count).T, preferred_element_type=jnp.float32)
    first = first.reshape(occ_count, virt_count, occ_count, virt_count)
    swapped = first.transpose(0, 3, 2, 1)
    denom = energy_own[:, None, None, None] + energy_part[None, None, :, None] - virt_energy[None, :, None, None] - virt_energy[None, None, None, :]
    tbar = ((2.0 * first - swapped) / denom).astype(jnp.bfloat16)
    flat = tbar.reshape(occ_count * virt_count, occ_count * virt_count)
    own = jnp.dot(flat, block_part.reshape(occ_count * virt_count, aux_count), preferred_element_type=jnp.float32)
    return flat, own.reshape(occ_count, virt_count, aux_count)


def partner_term(flat, block_own):
    occ_count, virt_count, aux_count = block_own.shape
    total = lax.dot_general(flat, block_own.reshape(occ_count * virt_count, aux_count), (((0,), (0,)), ((), ())), preferred_element_type=jnp.float32)
    return total.reshape(occ_count, virt_count, aux_count).astype(jnp.bfloat16)


def reference(three_index, occ_energy, virt_energy):
    owns = []
    partners = []
    for group in range(N_BLK):
        other = (group - 1) % N_BLK
        block_own = three_index[group * OCC_BLK:(group + 1) * OCC_BLK]
        block_part = three_index[other * OCC_BLK:(other + 1) * OCC_BLK]
        energy_own = occ_energy[group * OCC_BLK:(group + 1) * OCC_BLK]
        energy_part = occ_energy[other * OCC_BLK:(other + 1) * OCC_BLK]
        unused, diag_own = pair_terms(block_own, block_own, energy_own, energy_own, virt_energy)
        flat, cross_own = pair_terms(block_own, block_part, energy_own, energy_part, virt_energy)
        owns.append(diag_own + cross_own)
        partners.append(partner_term(flat, block_own))
    blocks = []
    for group in range(N_BLK):
        later = (group + 1) % N_BLK
        blocks.append((owns[group] + partners[later].astype(jnp.float32)).astype(jnp.bfloat16))
    return jnp.concatenate(blocks, axis=0)
```

```python
import functools

import jax
import jax.numpy as jnp
from jax import lax
from jax.experimental import pallas as pl
from jax.experimental.pallas import tpu as pltpu
from jax.sharding import PartitionSpec as P

MESH = pl.DeviceIdType.MESH
SEND_COLUMNS = 256
SUM_COLUMNS = 512


def shifted(shard, axis, by):
    devices = lax.axis_size(axis)
    return lax.ppermute(shard, axis, [(i, (i + by) % devices) for i in range(devices)])


def contract(left, right):
    return lax.dot_general(
        left, right, (((1,), (1,)), ((), ())), preferred_element_type=jnp.float32
    )


def plain_local(three_index, occ_energy, virt_energy):
    occ, rows, aux = three_index.shape
    virt = virt_energy.shape[0]
    energy_rows = lax.dynamic_slice_in_dim(virt_energy, lax.axis_index("virt") * rows, rows, 0)
    part_rows = shifted(three_index, "blk", 1)
    own_full = lax.all_gather(three_index, "virt", axis=1, tiled=True)
    part_full = shifted(own_full, "blk", 1)
    energy_part = shifted(occ_energy, "blk", 1)

    def pairs(left, right):
        both = contract(left.reshape(occ * rows, aux), right.reshape(occ * virt, aux))
        return both.reshape(occ, rows, occ, virt)

    def denominator(left, right):
        return (
            left[:, None, None, None]
            + right[None, None, :, None]
            - energy_rows[None, :, None, None]
            - virt_energy[None, None, None, :]
        )

    def spread(tbar, full):
        return jnp.dot(
            tbar.astype(jnp.bfloat16).reshape(occ * rows, occ * virt),
            full.reshape(occ * virt, aux),
            preferred_element_type=jnp.float32,
        ).reshape(occ, rows, aux)

    diag = pairs(three_index, own_full)
    first = pairs(three_index, part_full)
    second = pairs(part_rows, own_full)
    own = spread(
        (2.0 * diag - diag.transpose(2, 1, 0, 3)) / denominator(occ_energy, occ_energy), own_full
    )
    own += spread(
        (2.0 * first - second.transpose(2, 1, 0, 3)) / denominator(occ_energy, energy_part),
        part_full,
    )
    partner = spread(
        (2.0 * second - first.transpose(2, 1, 0, 3)) / denominator(energy_part, occ_energy),
        own_full,
    ).astype(jnp.bfloat16)
    partner = shifted(partner, "blk", -1)
    return (own + partner.astype(jnp.float32)).astype(jnp.bfloat16)


def kernel(
    members,
    blocks,
    a_ref,
    e_ref,
    column_ref,
    row_ref,
    o_ref,
    own_full,
    part_full,
    e_part,
    acc,
    pacc,
    psend,
    precv,
    k_ref,
    x_ref,
    tu_ref,
    t_ref,
    send_up,
    send_down,
    send_next,
    recv_own,
    recv_part,
    send_back,
    recv_back,
    e_sems,
    local_sem,
):
    occ, rows, aux = a_ref.shape
    size = occ * rows
    v = lax.axis_index("virt")
    g = lax.axis_index("blk")
    after = lax.rem(g + 1, blocks)
    before = lax.rem(g + blocks - 1, blocks)
    has_up = v + 1 < members
    has_down = v > 0

    def copy_up(src, s, c):
        return pltpu.make_async_remote_copy(
            src_ref=src, dst_ref=own_full.at[s, c], send_sem=send_up.at[s, c],
            recv_sem=recv_own.at[s, c], device_id={"virt": v + 1}, device_id_type=MESH,
        )

    def copy_down(src, s, c):
        return pltpu.make_async_remote_copy(
            src_ref=src, dst_ref=own_full.at[s, c], send_sem=send_down.at[s, c],
            recv_sem=recv_own.at[s, c], device_id={"virt": v - 1}, device_id_type=MESH,
        )

    def copy_next(src, s, c):
        return pltpu.make_async_remote_copy(
            src_ref=src, dst_ref=part_full.at[s, c], send_sem=send_next.at[s, c],
            recv_sem=recv_part.at[s, c], device_id={"blk": after}, device_id_type=MESH,
        )

    def arrived_own(s, c):
        return pltpu.make_async_remote_copy(
            src_ref=own_full.at[s, c], dst_ref=own_full.at[s, c], send_sem=send_next.at[s, c],
            recv_sem=recv_own.at[s, c], device_id={"blk": after}, device_id_type=MESH,
        )

    def copy_back(k):
        return pltpu.make_async_remote_copy(
            src_ref=psend.at[k], dst_ref=precv.at[k], send_sem=send_back.at[k],
            recv_sem=recv_back.at[k], device_id={"blk": before}, device_id_type=MESH,
        )

    energy_copy = pltpu.make_async_remote_copy(
        src_ref=e_ref, dst_ref=e_part, send_sem=e_sems.at[0], recv_sem=e_sems.at[1],
        device_id={"blk": after}, device_id_type=MESH,
    )
    keep = pltpu.make_async_copy(a_ref, own_full.at[v], local_sem)

    barrier = pltpu.get_barrier_semaphore()
    pl.semaphore_signal(barrier, inc=1, device_id={"blk": after}, device_id_type=MESH)
    pl.semaphore_signal(barrier, inc=1, device_id={"blk": before}, device_id_type=MESH)

    @pl.when(has_up)
    def _():
        pl.semaphore_signal(barrier, inc=1, device_id={"virt": v + 1}, device_id_type=MESH)

    @pl.when(has_down)
    def _():
        pl.semaphore_signal(barrier, inc=1, device_id={"virt": v - 1}, device_id_type=MESH)

    pl.semaphore_wait(barrier, 2 + has_up.astype(jnp.int32) + has_down.astype(jnp.int32))

    energy_copy.start()
    for c in range(occ):
        @pl.when(has_up)
        def _():
            copy_up(a_ref.at[c], v, c).start()

        @pl.when(has_down)
        def _():
            copy_down(a_ref.at[c], v, c).start()

        copy_next(a_ref.at[c], v, c).start()
    keep.start()
    acc[...] = jnp.zeros_like(acc)
    pacc[...] = jnp.zeros_like(pacc)
    keep.wait()
    energy_copy.wait_recv()

    def inverse(left, i, right, j, s):
        own_rows = column_ref[pl.ds(pl.multiple_of(v * rows, rows), rows), :]
        return 1.0 / ((left[i : i + 1, 0:1] + right[j : j + 1, 0:1]) - own_rows - row_ref[s])

    def at(i):
        return slice(i * rows, (i + 1) * rows)

    def add_columns(total, left, source, s, width):
        @pl.loop(0, aux // width)
        def _(k):
            cols = pl.ds(pl.multiple_of(k * width, width), width)
            total[:, cols] += jnp.dot(
                left[...], source[s, :, :, cols].reshape(size, width),
                preferred_element_type=jnp.float32,
            )

    last = jnp.where(2 * v > members - 1, 0, members - 1)

    def compute(s):
        own = own_full[s].reshape(size, aux)
        k_ref[...] = contract(a_ref[...].reshape(size, aux), own)
        for i in range(occ):
            for j in range(occ):
                tu_ref[at(i), at(j)] = (
                    (2.0 * k_ref[at(i), at(j)] - k_ref[at(j), at(i)])
                    * inverse(e_ref, i, e_ref, j, s)
                ).astype(jnp.bfloat16)
        add_columns(acc, tu_ref, own_full, s, SUM_COLUMNS)

        @pl.when(s == v)
        def _():
            for c in range(occ):
                copy_next(part_full.at[s, c], s, c).wait_recv()

        k_ref[...] = contract(part_full[v].reshape(size, aux), own_full[s].reshape(size, aux))

        @pl.when(s != v)
        def _():
            for c in range(occ):
                copy_next(part_full.at[s, c], s, c).wait_recv()

        x_ref[...] = contract(a_ref[...].reshape(size, aux), part_full[s].reshape(size, aux))
        for i in range(occ):
            for j in range(occ):
                scale = inverse(e_ref, i, e_part, j, s)
                x = x_ref[at(i), at(j)]
                y = k_ref[at(j), at(i)]
                t_ref[at(i), at(j)] = ((2.0 * x - y) * scale).astype(jnp.bfloat16)
                tu_ref[at(j), at(i)] = ((2.0 * y - x) * scale).astype(jnp.bfloat16)

        @pl.when(s != last)
        def _():
            add_columns(pacc, tu_ref, own_full, s, SUM_COLUMNS)
            add_columns(acc, t_ref, part_full, s, SUM_COLUMNS)

    def level(d, carry):
        @pl.when(d > 0)
        def _():
            for c in range(occ):
                below, above = v - d, v + d

                @pl.when(below >= 0)
                def _():
                    arrived_own(below, c).wait_recv()

                    @pl.when(has_up)
                    def _():
                        copy_up(own_full.at[below, c], below, c).start()

                    copy_next(own_full.at[below, c], below, c).start()

                @pl.when(above < members)
                def _():
                    arrived_own(above, c).wait_recv()

                    @pl.when(has_down)
                    def _():
                        copy_down(own_full.at[above, c], above, c).start()

                    copy_next(own_full.at[above, c], above, c).start()

        def side(t, inner):
            s = v - d + 2 * d * t

            @pl.when((s >= 0) & (s < members) & (d + (1 - t) > 0))
            def _():
                compute(s)

            return inner

        return lax.fori_loop(0, 2, side, carry)

    lax.fori_loop(0, members, level, 0)

    for k in range(aux // SEND_COLUMNS):
        cols = slice(k * SEND_COLUMNS, (k + 1) * SEND_COLUMNS)
        psend[k] = (
            pacc[:, cols]
            + jnp.dot(
                tu_ref[...], own_full[last, :, :, cols].reshape(size, SEND_COLUMNS),
                preferred_element_type=jnp.float32,
            )
        ).astype(jnp.bfloat16)
        copy_back(k).start()
    add_columns(acc, t_ref, part_full, last, SUM_COLUMNS)
    for k in range(aux // SEND_COLUMNS):
        cols = slice(k * SEND_COLUMNS, (k + 1) * SEND_COLUMNS)
        copy_back(k).wait_recv()
        o_ref[:, :, cols] = (
            (acc[:, cols] + precv[k].astype(jnp.float32))
            .astype(jnp.bfloat16)
            .reshape(occ, rows, SEND_COLUMNS)
        )

    energy_copy.wait_send()
    for k in range(aux // SEND_COLUMNS):
        copy_back(k).wait_send()

    def drain(s, carry):
        for c in range(occ):
            copy_next(own_full.at[s, c], s, c).wait_send()

            @pl.when(has_up & (s <= v))
            def _():
                copy_up(own_full.at[s, c], s, c).wait_send()

            @pl.when(has_down & (s >= v))
            def _():
                copy_down(own_full.at[s, c], s, c).wait_send()

        return carry

    lax.fori_loop(0, members, drain, 0)


def fused_local(three_index, occ_energy, virt_energy):
    occ, rows, aux = three_index.shape
    members, blocks = lax.axis_size("virt"), lax.axis_size("blk")
    size, parts = occ * rows, aux // SEND_COLUMNS
    energies = jnp.broadcast_to(occ_energy[:, None], (occ, 128))
    vmem = pl.BlockSpec(memory_space=pltpu.VMEM)
    dma = pltpu.SemaphoreType.DMA
    return pl.pallas_call(
        functools.partial(kernel, members, blocks),
        out_shape=jax.ShapeDtypeStruct((occ, rows, aux), jnp.bfloat16),
        in_specs=[vmem] * 4,
        out_specs=vmem,
        scratch_shapes=[
            pltpu.VMEM((members, occ, rows, aux), jnp.bfloat16),
            pltpu.VMEM((members, occ, rows, aux), jnp.bfloat16),
            pltpu.VMEM((occ, 128), jnp.float32),
            pltpu.VMEM((size, aux), jnp.float32),
            pltpu.VMEM((size, aux), jnp.float32),
            pltpu.VMEM((parts, size, SEND_COLUMNS), jnp.bfloat16),
            pltpu.VMEM((parts, size, SEND_COLUMNS), jnp.bfloat16),
            pltpu.VMEM((size, size), jnp.float32),
            pltpu.VMEM((size, size), jnp.float32),
            pltpu.VMEM((size, size), jnp.bfloat16),
            pltpu.VMEM((size, size), jnp.bfloat16),
            dma((members, occ)),
            dma((members, occ)),
            dma((members, occ)),
            dma((members, occ)),
            dma((members, occ)),
            dma((parts,)),
            dma((parts,)),
            dma((2,)),
            dma,
        ],
        compiler_params=pltpu.CompilerParams(
            collective_id=0, has_side_effects=True, vmem_limit_bytes=62 * 2**20
        ),
    )(
        three_index,
        energies,
        virt_energy[:, None],
        virt_energy.reshape(members, 1, rows),
    )


def local(three_index, occ_energy, virt_energy):
    occ, rows, aux = three_index.shape
    if rows % 128 == 0 and aux % SUM_COLUMNS == 0:
        return fused_local(three_index, occ_energy, virt_energy)
    return plain_local(three_index, occ_energy, virt_energy)


def solution(mesh):
    placed = (P(("copies", "blk"), "virt", None), P(("copies", "blk")), P("copies"))
    return jax.shard_map(
        local,
        mesh=mesh,
        in_specs=placed,
        out_specs=P(("copies", "blk"), "virt", None),
        check_vma=False,
    )
```

```python
import functools

import jax
import jax.numpy as jnp
from jax import lax
from jax.experimental import pallas as pl
from jax.experimental.pallas import tpu as pltpu
from jax.sharding import PartitionSpec as P

MESH = pl.DeviceIdType.MESH
SEND_COLUMNS = 256
SUM_COLUMNS = 512


def shifted(shard, axis, by):
    devices = lax.axis_size(axis)
    return lax.ppermute(shard, axis, [(i, (i + by) % devices) for i in range(devices)])


def contract(left, right):
    return lax.dot_general(
        left, right, (((1,), (1,)), ((), ())), preferred_element_type=jnp.float32
    )


def plain_local(three_index, occ_energy, virt_energy):
    occ, rows, aux = three_index.shape
    virt = virt_energy.shape[0]
    energy_rows = lax.dynamic_slice_in_dim(virt_energy, lax.axis_index("virt") * rows, rows, 0)
    part_rows = shifted(three_index, "blk", 1)
    own_full = lax.all_gather(three_index, "virt", axis=1, tiled=True)
    part_full = shifted(own_full, "blk", 1)
    energy_part = shifted(occ_energy, "blk", 1)

    def pairs(left, right):
        both = contract(left.reshape(occ * rows, aux), right.reshape(occ * virt, aux))
        return both.reshape(occ, rows, occ, virt)

    def denominator(left, right):
        return (
            left[:, None, None, None]
            + right[None, None, :, None]
            - energy_rows[None, :, None, None]
            - virt_energy[None, None, None, :]
        )

    def spread(tbar, full):
        return jnp.dot(
            tbar.astype(jnp.bfloat16).reshape(occ * rows, occ * virt),
            full.reshape(occ * virt, aux),
            preferred_element_type=jnp.float32,
        ).reshape(occ, rows, aux)

    diag = pairs(three_index, own_full)
    first = pairs(three_index, part_full)
    second = pairs(part_rows, own_full)
    own = spread(
        (2.0 * diag - diag.transpose(2, 1, 0, 3)) / denominator(occ_energy, occ_energy), own_full
    )
    own += spread(
        (2.0 * first - second.transpose(2, 1, 0, 3)) / denominator(occ_energy, energy_part),
        part_full,
    )
    partner = spread(
        (2.0 * second - first.transpose(2, 1, 0, 3)) / denominator(energy_part, occ_energy),
        own_full,
    ).astype(jnp.bfloat16)
    partner = shifted(partner, "blk", -1)
    return (own + partner.astype(jnp.float32)).astype(jnp.bfloat16)


def kernel(
    blocks,
    a_ref,
    e_ref,
    row_ref,
    o_ref,
    own_full,
    part_full,
    e_part,
    column_ref,
    acc,
    pacc,
    racc,
    psend,
    precv,
    hsend,
    hrecv,
    rsend,
    rrecv,
    k_ref,
    x_ref,
    tu_ref,
    t_ref,
    send_in,
    send_out,
    send_next,
    recv_own,
    recv_part,
    back_sems,
    help_sems,
    result_sems,
    e_sems,
    local_sem,
):
    occ, rows, aux = a_ref.shape
    size = occ * rows
    half = occ // 2
    chunks = range(aux // SEND_COLUMNS)
    v = lax.axis_index("virt")
    g = lax.axis_index("blk")
    after = lax.rem(g + 1, blocks)
    before = lax.rem(g + blocks - 1, blocks)
    step = jnp.where(v < 2, 1, -1)
    middle = (v == 1) | (v == 2)
    end = (v == 0) | (v == 3)
    inner = v + step
    outer = lax.rem(v - step + 4, 4)
    far = lax.rem(v + 2 * step + 4, 4)
    near = jnp.where(middle, outer, inner)
    last = jnp.where(middle, inner, far)

    def remote(src, dst, send, recv, **where):
        return pltpu.make_async_remote_copy(
            src_ref=src, dst_ref=dst, send_sem=send, recv_sem=recv,
            device_id=where, device_id_type=MESH,
        )

    def to_inner(s, c):
        return remote(
            own_full.at[s, c], own_full.at[s, c], send_in.at[s, c], recv_own.at[s, c], virt=inner
        )

    def to_outer(s, c):
        return remote(
            own_full.at[s, c], own_full.at[s, c], send_out.at[s, c], recv_own.at[s, c], virt=outer
        )

    def to_next(s, c):
        return remote(
            own_full.at[s, c], part_full.at[s, c], send_next.at[s, c], recv_part.at[s, c],
            blk=after,
        )

    def back(k):
        return remote(
            psend.at[k], precv.at[k], back_sems.at[0, k], back_sems.at[1, k], blk=before
        )

    def help_back(k):
        return remote(
            hsend.at[k], hrecv.at[k], help_sems.at[0, k], help_sems.at[1, k], blk=before
        )

    def result(k):
        return remote(
            rsend.at[k], rrecv.at[k], result_sems.at[0, k], result_sems.at[1, k], virt=outer
        )

    def own_copy(make, send, c):
        return remote(
            a_ref.at[c], make.at[v, c], send.at[v, c],
            (recv_part if make is part_full else recv_own).at[v, c],
            **({"blk": after} if make is part_full else {"virt": inner if send is send_in else outer}),
        )

    energy_copy = remote(e_ref, e_part, e_sems.at[0], e_sems.at[1], blk=after)
    keep = pltpu.make_async_copy(a_ref, own_full.at[v], local_sem)

    barrier = pltpu.get_barrier_semaphore()
    pl.semaphore_signal(barrier, inc=1, device_id={"blk": after}, device_id_type=MESH)
    pl.semaphore_signal(barrier, inc=1, device_id={"blk": before}, device_id_type=MESH)
    pl.semaphore_signal(barrier, inc=1, device_id={"virt": inner}, device_id_type=MESH)

    @pl.when(middle)
    def _():
        pl.semaphore_signal(barrier, inc=1, device_id={"virt": outer}, device_id_type=MESH)

    pl.semaphore_wait(barrier, 3 + middle.astype(jnp.int32))

    for c in range(half):
        own_copy(own_full, send_in, c).start()
    for c in range(half, occ):
        @pl.when(end)
        def _():
            own_copy(own_full, send_in, c).start()
    for c in range(occ):
        @pl.when(middle)
        def _():
            own_copy(own_full, send_out, c).start()
    energy_copy.start()
    for c in range(occ):
        own_copy(part_full, send_next, c).start()
    keep.start()
    for s in range(4):
        column_ref[s] = jnp.transpose(jnp.broadcast_to(row_ref[s], (rows, rows)))[:, 0:1]
    keep.wait()

    def inverse(left, i, right, j, r, s):
        return 1.0 / (
            (left[0:1, i : i + 1] + right[0:1, j : j + 1]) - column_ref[r] - row_ref[s]
        )

    def at(i):
        return slice(i * rows, (i + 1) * rows)

    def product(left, source, s, cols, width):
        return jnp.dot(
            left[...], source[s, :, :, cols].reshape(size, width),
            preferred_element_type=jnp.float32,
        )

    def add_columns(total, left, source, s, first):
        @pl.loop(0, aux // SUM_COLUMNS)
        def _(k):
            cols = pl.ds(pl.multiple_of(k * SUM_COLUMNS, SUM_COLUMNS), SUM_COLUMNS)
            value = product(left, source, s, cols, SUM_COLUMNS)
            if first:
                total[:, cols] = value
            else:
                total[:, cols] += value

    def shard(source, s):
        return source[s].reshape(size, aux)

    def part_arrives(s):
        for c in range(occ):
            to_next(s, c).wait_recv()

    def diagonal(r, s, total, first):
        k_ref[...] = contract(shard(own_full, r), shard(own_full, s))
        for i in range(occ):
            for j in range(occ):
                tu_ref[at(i), at(j)] = (
                    (2.0 * k_ref[at(i), at(j)] - k_ref[at(j), at(i)])
                    * inverse(e_ref, i, e_ref, j, r, s)
                ).astype(jnp.bfloat16)
        add_columns(total, tu_ref, own_full, s, first)

    def cross(r, s, same):
        if same:
            part_arrives(s)
        k_ref[...] = contract(shard(part_full, r), shard(own_full, s))
        if same is False:
            part_arrives(s)
        x_ref[...] = contract(shard(own_full, r), shard(part_full, s))
        amplitudes(r, s)

    def amplitudes(r, s):
        for i in range(occ):
            for j in range(occ):
                scale = inverse(e_ref, i, e_part, j, r, s)
                x = x_ref[at(i), at(j)]
                y = k_ref[at(j), at(i)]
                t_ref[at(i), at(j)] = ((2.0 * x - y) * scale).astype(jnp.bfloat16)
                tu_ref[at(j), at(i)] = ((2.0 * y - x) * scale).astype(jnp.bfloat16)

    def spread(s, first):
        add_columns(pacc, tu_ref, own_full, s, first)
        add_columns(acc, t_ref, part_full, s, False)

    def from_outer(c):
        to_outer(outer, c).wait_recv()
        to_inner(outer, c).start()
        to_next(outer, c).start()

    def from_partner(c, forward):
        to_inner(inner, c).wait_recv()
        to_outer(inner, c).start()
        if forward:
            to_next(inner, c).start()

    def from_far(c):
        to_inner(far, c).wait_recv()
        to_next(far, c).start()

    def from_inner(s, c):
        to_inner(s, c).wait_recv()
        to_next(s, c).start()

    diagonal(v, v, acc, True)
    energy_copy.wait_recv()

    for c in range(half):
        @pl.when(middle)
        def _():
            from_outer(c)
            from_partner(c, False)

        @pl.when(end)
        def _():
            from_inner(inner, c)

    cross(v, v, True)
    spread(v, True)

    for c in range(half, occ):
        @pl.when(middle)
        def _():
            from_outer(c)

        @pl.when(end)
        def _():
            from_inner(inner, c)

    @pl.when(middle)
    def _():
        for c in range(half, occ):
            own_copy(own_full, send_in, c).start()
        for c in range(half):
            from_far(c)

    diagonal(v, near, acc, False)

    @pl.when(middle)
    def _():
        for c in range(half, occ - 1):
            from_far(c)

    cross(v, near, False)
    spread(near, False)

    @pl.when(middle)
    def _():
        from_far(occ - 1)
        for c in range(half):
            to_next(inner, c).start()
        diagonal(outer, far, racc, True)
        cross(outer, far, False)
        for k in chunks:
            cols = slice(k * SEND_COLUMNS, (k + 1) * SEND_COLUMNS)
            hsend[k] = product(tu_ref, own_full, far, cols, SEND_COLUMNS).astype(jnp.bfloat16)
            help_back(k).start()
        for c in range(half, occ - 1):
            from_partner(c, True)
        add_columns(racc, t_ref, part_full, far, False)
        from_partner(occ - 1, True)
        for k in chunks:
            cols = slice(k * SEND_COLUMNS, (k + 1) * SEND_COLUMNS)
            help_back(k).wait_recv()
            rsend[k] = (racc[:, cols] + hrecv[k].astype(jnp.float32)).astype(jnp.bfloat16)
            result(k).start()
        diagonal(v, far, acc, False)
        cross(v, far, None)
        spread(far, False)

    @pl.when(end)
    def _():
        for c in range(occ):
            from_inner(far, c)

    diagonal(v, last, acc, False)
    cross(v, last, False)
    for k in chunks:
        cols = slice(k * SEND_COLUMNS, (k + 1) * SEND_COLUMNS)
        psend[k] = (
            pacc[:, cols] + product(tu_ref, own_full, last, cols, SEND_COLUMNS)
        ).astype(jnp.bfloat16)
        back(k).start()
    add_columns(acc, t_ref, part_full, last, False)
    for k in chunks:
        cols = slice(k * SEND_COLUMNS, (k + 1) * SEND_COLUMNS)

        @pl.when(end)
        def _():
            result(k).wait_recv()
            acc[:, cols] += rrecv[k].astype(jnp.float32)

        back(k).wait_recv()
        o_ref[:, :, cols] = (
            (acc[:, cols] + precv[k].astype(jnp.float32))
            .astype(jnp.bfloat16)
            .reshape(occ, rows, SEND_COLUMNS)
        )

    energy_copy.wait_send()
    for k in chunks:
        back(k).wait_send()
    for c in range(occ):
        for s in (v, inner, far):
            to_next(s, c).wait_send()
        to_inner(v, c).wait_send()

        @pl.when(middle)
        def _():
            to_next(outer, c).wait_send()
            to_inner(outer, c).wait_send()
            to_outer(v, c).wait_send()
            to_outer(inner, c).wait_send()

    @pl.when(middle)
    def _():
        for k in chunks:
            help_back(k).wait_send()
            result(k).wait_send()


def fused_local(three_index, occ_energy, virt_energy):
    occ, rows, aux = three_index.shape
    members, blocks = lax.axis_size("virt"), lax.axis_size("blk")
    size, parts = occ * rows, aux // SEND_COLUMNS
    vmem = pl.BlockSpec(memory_space=pltpu.VMEM)
    dma = pltpu.SemaphoreType.DMA
    full = pltpu.VMEM((members, occ, rows, aux), jnp.bfloat16)
    total = pltpu.VMEM((size, aux), jnp.float32)
    pieces = pltpu.VMEM((parts, size, SEND_COLUMNS), jnp.bfloat16)
    return pl.pallas_call(
        functools.partial(kernel, blocks),
        out_shape=jax.ShapeDtypeStruct((occ, rows, aux), jnp.bfloat16),
        in_specs=[vmem] * 3,
        out_specs=vmem,
        scratch_shapes=[
            full,
            full,
            pltpu.VMEM((1, occ), jnp.float32),
            pltpu.VMEM((members, rows, 1), jnp.float32),
            *[total] * 3,
            *[pieces] * 6,
            *[pltpu.VMEM((size, size), jnp.float32)] * 2,
            *[pltpu.VMEM((size, size), jnp.bfloat16)] * 2,
            *[dma((members, occ))] * 5,
            *[dma((2, parts))] * 3,
            dma((2,)),
            dma,
        ],
        compiler_params=pltpu.CompilerParams(
            collective_id=0, has_side_effects=True, vmem_limit_bytes=63 * 2**20
        ),
    )(three_index, occ_energy.reshape(1, occ), virt_energy.reshape(members, 1, rows))


def local(three_index, occ_energy, virt_energy):
    occ, rows, aux = three_index.shape
    tiles = rows % 128 == 0 and aux % SUM_COLUMNS == 0 and occ % 2 == 0
    if tiles and lax.axis_size("virt") == 4:
        return fused_local(three_index, occ_energy, virt_energy)
    return plain_local(three_index, occ_energy, virt_energy)


def solution(mesh):
    placed = (P(("copies", "blk"), "virt", None), P(("copies", "blk")), P("copies"))
    return jax.shard_map(
        local,
        mesh=mesh,
        in_specs=placed,
        out_specs=P(("copies", "blk"), "virt", None),
        check_vma=False,
    )
```

```python
import functools

import jax
import jax.numpy as jnp
from jax import lax
from jax.experimental import pallas as pl
from jax.experimental.pallas import tpu as pltpu
from jax.sharding import PartitionSpec as P

MESH = pl.DeviceIdType.MESH
SEND_COLUMNS = 256
SUM_COLUMNS = 512


def shifted(shard, axis, by):
    devices = lax.axis_size(axis)
    return lax.ppermute(shard, axis, [(i, (i + by) % devices) for i in range(devices)])


def contract(left, right):
    return lax.dot_general(
        left, right, (((1,), (1,)), ((), ())), preferred_element_type=jnp.float32
    )


def plain_local(three_index, occ_energy, virt_energy):
    occ, rows, aux = three_index.shape
    virt = virt_energy.shape[0]
    energy_rows = lax.dynamic_slice_in_dim(virt_energy, lax.axis_index("virt") * rows, rows, 0)
    part_rows = shifted(three_index, "blk", 1)
    own_full = lax.all_gather(three_index, "virt", axis=1, tiled=True)
    part_full = shifted(own_full, "blk", 1)
    energy_part = shifted(occ_energy, "blk", 1)

    def pairs(left, right):
        both = contract(left.reshape(occ * rows, aux), right.reshape(occ * virt, aux))
        return both.reshape(occ, rows, occ, virt)

    def denominator(left, right):
        return (
            left[:, None, None, None]
            + right[None, None, :, None]
            - energy_rows[None, :, None, None]
            - virt_energy[None, None, None, :]
        )

    def spread(tbar, full):
        return jnp.dot(
            tbar.astype(jnp.bfloat16).reshape(occ * rows, occ * virt),
            full.reshape(occ * virt, aux),
            preferred_element_type=jnp.float32,
        ).reshape(occ, rows, aux)

    diag = pairs(three_index, own_full)
    first = pairs(three_index, part_full)
    second = pairs(part_rows, own_full)
    own = spread(
        (2.0 * diag - diag.transpose(2, 1, 0, 3)) / denominator(occ_energy, occ_energy), own_full
    )
    own += spread(
        (2.0 * first - second.transpose(2, 1, 0, 3)) / denominator(occ_energy, energy_part),
        part_full,
    )
    partner = spread(
        (2.0 * second - first.transpose(2, 1, 0, 3)) / denominator(energy_part, occ_energy),
        own_full,
    ).astype(jnp.bfloat16)
    partner = shifted(partner, "blk", -1)
    return (own + partner.astype(jnp.float32)).astype(jnp.bfloat16)


def kernel(
    blocks,
    a_ref,
    e_ref,
    row_ref,
    o_ref,
    own_full,
    part_full,
    e_part,
    column_ref,
    acc,
    pacc,
    racc,
    psend,
    precv,
    hsend,
    hrecv,
    rsend,
    rrecv,
    k_ref,
    x_ref,
    td_ref,
    tu_ref,
    t_ref,
    staged,
    send_in,
    send_out,
    send_next,
    recv_own,
    recv_part,
    back_sems,
    help_sems,
    result_sems,
    e_sems,
    out_sems,
    local_sem,
):
    occ, rows, aux = a_ref.shape
    size = occ * rows
    half = occ // 2
    chunks = range(aux // SEND_COLUMNS)
    v = lax.axis_index("virt")
    g = lax.axis_index("blk")
    after = lax.rem(g + 1, blocks)
    before = lax.rem(g + blocks - 1, blocks)
    step = jnp.where(v < 2, 1, -1)
    middle = (v == 1) | (v == 2)
    end = (v == 0) | (v == 3)
    inner = v + step
    outer = lax.rem(v - step + 4, 4)
    far = lax.rem(v + 2 * step + 4, 4)
    near = jnp.where(middle, outer, inner)
    last = jnp.where(middle, inner, far)

    def remote(src, dst, send, recv, **where):
        return pltpu.make_async_remote_copy(
            src_ref=src, dst_ref=dst, send_sem=send, recv_sem=recv,
            device_id=where, device_id_type=MESH,
        )

    def to_inner(s, c):
        return remote(
            own_full.at[s, c], own_full.at[s, c], send_in.at[s, c], recv_own.at[s, c], virt=inner
        )

    def to_outer(s, c):
        return remote(
            own_full.at[s, c], own_full.at[s, c], send_out.at[s, c], recv_own.at[s, c], virt=outer
        )

    def to_next(s, c):
        return remote(
            own_full.at[s, c], part_full.at[s, c], send_next.at[s, c], recv_part.at[s, c],
            blk=after,
        )

    def back(k):
        return remote(
            psend.at[k], precv.at[k], back_sems.at[0, k], back_sems.at[1, k], blk=before
        )

    def help_back(k):
        return remote(
            hsend.at[k], hrecv.at[k], help_sems.at[0, k], help_sems.at[1, k], blk=before
        )

    def result(k):
        return remote(
            rsend.at[k], rrecv.at[k], result_sems.at[0, k], result_sems.at[1, k], virt=outer
        )

    def own_copy(make, send, c):
        return remote(
            a_ref.at[c], make.at[v, c], send.at[v, c],
            (recv_part if make is part_full else recv_own).at[v, c],
            **({"blk": after} if make is part_full else {"virt": inner if send is send_in else outer}),
        )

    def write(k):
        cols = slice(k * SEND_COLUMNS, (k + 1) * SEND_COLUMNS)
        return pltpu.make_async_copy(staged.at[k], o_ref.at[:, :, cols], out_sems.at[k])

    energy_copy = remote(e_ref, e_part, e_sems.at[0], e_sems.at[1], blk=after)
    keep = pltpu.make_async_copy(a_ref, own_full.at[v], local_sem)

    barrier = pltpu.get_barrier_semaphore()
    pl.semaphore_signal(barrier, inc=1, device_id={"blk": after}, device_id_type=MESH)
    pl.semaphore_signal(barrier, inc=1, device_id={"blk": before}, device_id_type=MESH)
    pl.semaphore_signal(barrier, inc=1, device_id={"virt": inner}, device_id_type=MESH)

    @pl.when(middle)
    def _():
        pl.semaphore_signal(barrier, inc=1, device_id={"virt": outer}, device_id_type=MESH)

    pl.semaphore_wait(barrier, 3 + middle.astype(jnp.int32))

    for c in range(half):
        own_copy(own_full, send_in, c).start()
    for c in range(half, occ):
        @pl.when(end)
        def _():
            own_copy(own_full, send_in, c).start()
    for c in range(occ):
        @pl.when(middle)
        def _():
            own_copy(own_full, send_out, c).start()
    energy_copy.start()
    for c in range(occ):
        own_copy(part_full, send_next, c).start()
    keep.start()
    for s in range(4):
        column_ref[s] = jnp.transpose(jnp.broadcast_to(row_ref[s], (rows, rows)))[:, 0:1]
    keep.wait()

    def inverse(left, i, right, j, r, s):
        return 1.0 / (
            (left[0:1, i : i + 1] + right[0:1, j : j + 1]) - column_ref[r] - row_ref[s]
        )

    def at(i):
        return slice(i * rows, (i + 1) * rows)

    def product(left, source, s, cols, width):
        return jnp.dot(
            left[...], source[s, :, :, cols].reshape(size, width),
            preferred_element_type=jnp.float32,
        )

    def add_columns(total, left, source, s, first):
        @pl.loop(0, aux // SUM_COLUMNS)
        def _(k):
            cols = pl.ds(pl.multiple_of(k * SUM_COLUMNS, SUM_COLUMNS), SUM_COLUMNS)
            value = product(left, source, s, cols, SUM_COLUMNS)
            if first:
                total[:, cols] = value
            else:
                total[:, cols] += value

    def shard(source, s):
        return source[s].reshape(size, aux)

    def part_arrives(s):
        for c in range(occ):
            to_next(s, c).wait_recv()

    def pair_ratio(r, s, ratio_ref):
        k_ref[...] = contract(shard(own_full, r), shard(own_full, s))
        for i in range(occ):
            for j in range(occ):
                ratio_ref[at(i), at(j)] = (
                    (2.0 * k_ref[at(i), at(j)] - k_ref[at(j), at(i)])
                    * inverse(e_ref, i, e_ref, j, r, s)
                ).astype(jnp.bfloat16)

    def diagonal(r, s, total, first):
        pair_ratio(r, s, tu_ref)
        add_columns(total, tu_ref, own_full, s, first)

    def cross(r, s, same):
        if same:
            part_arrives(s)
        k_ref[...] = contract(shard(part_full, r), shard(own_full, s))
        if same is False:
            part_arrives(s)
        x_ref[...] = contract(shard(own_full, r), shard(part_full, s))
        amplitudes(r, s)

    def amplitudes(r, s):
        for i in range(occ):
            for j in range(occ):
                scale = inverse(e_ref, i, e_part, j, r, s)
                x = x_ref[at(i), at(j)]
                y = k_ref[at(j), at(i)]
                t_ref[at(i), at(j)] = ((2.0 * x - y) * scale).astype(jnp.bfloat16)
                tu_ref[at(j), at(i)] = ((2.0 * y - x) * scale).astype(jnp.bfloat16)

    def spread(s, first):
        add_columns(pacc, tu_ref, own_full, s, first)
        add_columns(acc, t_ref, part_full, s, False)

    def from_outer(c):
        to_outer(outer, c).wait_recv()
        to_inner(outer, c).start()
        to_next(outer, c).start()

    def from_partner(c, forward):
        to_inner(inner, c).wait_recv()
        to_outer(inner, c).start()
        if forward:
            to_next(inner, c).start()

    def from_far(c):
        to_inner(far, c).wait_recv()
        to_next(far, c).start()

    def from_inner(s, c):
        to_inner(s, c).wait_recv()
        to_next(s, c).start()

    diagonal(v, v, acc, True)
    energy_copy.wait_recv()

    for c in range(half):
        @pl.when(middle)
        def _():
            from_outer(c)
            from_partner(c, False)

        @pl.when(end)
        def _():
            from_inner(inner, c)

    cross(v, v, True)
    spread(v, True)

    for c in range(half, occ):
        @pl.when(middle)
        def _():
            from_outer(c)

        @pl.when(end)
        def _():
            from_inner(inner, c)

    @pl.when(middle)
    def _():
        for c in range(half, occ):
            own_copy(own_full, send_in, c).start()
        for c in range(half):
            from_far(c)

    diagonal(v, near, acc, False)

    @pl.when(middle)
    def _():
        for c in range(half, occ - 1):
            from_far(c)

    cross(v, near, False)
    spread(near, False)

    @pl.when(middle)
    def _():
        from_far(occ - 1)
        for c in range(half):
            to_next(inner, c).start()
        pair_ratio(outer, far, td_ref)
        cross(outer, far, False)
        for k in chunks:
            cols = slice(k * SEND_COLUMNS, (k + 1) * SEND_COLUMNS)
            hsend[k] = product(tu_ref, own_full, far, cols, SEND_COLUMNS).astype(jnp.bfloat16)
            help_back(k).start()
        for c in range(half, occ - 1):
            from_partner(c, True)

        @pl.loop(0, aux // SUM_COLUMNS)
        def _(k):
            cols = pl.ds(pl.multiple_of(k * SUM_COLUMNS, SUM_COLUMNS), SUM_COLUMNS)
            racc[:, cols] = product(td_ref, own_full, far, cols, SUM_COLUMNS) + product(
                t_ref, part_full, far, cols, SUM_COLUMNS
            )

        diagonal(v, far, acc, False)
        from_partner(occ - 1, True)
        for k in chunks:
            cols = slice(k * SEND_COLUMNS, (k + 1) * SEND_COLUMNS)
            help_back(k).wait_recv()
            rsend[k] = (racc[:, cols] + hrecv[k].astype(jnp.float32)).astype(jnp.bfloat16)
            result(k).start()
        cross(v, far, None)
        spread(far, False)

    @pl.when(end)
    def _():
        for c in range(occ):
            from_inner(far, c)

    diagonal(v, last, acc, False)
    cross(v, last, False)
    for k in chunks:
        cols = slice(k * SEND_COLUMNS, (k + 1) * SEND_COLUMNS)
        psend[k] = (
            pacc[:, cols] + product(tu_ref, own_full, last, cols, SEND_COLUMNS)
        ).astype(jnp.bfloat16)
        back(k).start()
    add_columns(acc, t_ref, part_full, last, False)
    for k in chunks:
        cols = slice(k * SEND_COLUMNS, (k + 1) * SEND_COLUMNS)

        @pl.when(end)
        def _():
            result(k).wait_recv()
            acc[:, cols] += rrecv[k].astype(jnp.float32)

        back(k).wait_recv()
        staged[k] = (
            (acc[:, cols] + precv[k].astype(jnp.float32))
            .astype(jnp.bfloat16)
            .reshape(occ, rows, SEND_COLUMNS)
        )
        write(k).start()

    energy_copy.wait_send()
    for k in chunks:
        back(k).wait_send()
        write(k).wait()
    for c in range(occ):
        for s in (v, inner, far):
            to_next(s, c).wait_send()
        to_inner(v, c).wait_send()

        @pl.when(middle)
        def _():
            to_next(outer, c).wait_send()
            to_inner(outer, c).wait_send()
            to_outer(v, c).wait_send()
            to_outer(inner, c).wait_send()

    @pl.when(middle)
    def _():
        for k in chunks:
            help_back(k).wait_send()
            result(k).wait_send()


def fused_local(three_index, occ_energy, virt_energy):
    occ, rows, aux = three_index.shape
    members, blocks = lax.axis_size("virt"), lax.axis_size("blk")
    size, parts = occ * rows, aux // SEND_COLUMNS
    vmem = pl.BlockSpec(memory_space=pltpu.VMEM)
    dma = pltpu.SemaphoreType.DMA
    full = pltpu.VMEM((members, occ, rows, aux), jnp.bfloat16)
    total = pltpu.VMEM((size, aux), jnp.float32)
    pieces = pltpu.VMEM((parts, size, SEND_COLUMNS), jnp.bfloat16)
    return pl.pallas_call(
        functools.partial(kernel, blocks),
        out_shape=jax.ShapeDtypeStruct((occ, rows, aux), jnp.bfloat16),
        in_specs=[pl.BlockSpec(memory_space=pl.ANY), vmem, vmem],
        out_specs=pl.BlockSpec(memory_space=pl.ANY),
        scratch_shapes=[
            full,
            full,
            pltpu.VMEM((1, occ), jnp.float32),
            pltpu.VMEM((members, rows, 1), jnp.float32),
            *[total] * 3,
            *[pieces] * 6,
            *[pltpu.VMEM((size, size), jnp.float32)] * 2,
            *[pltpu.VMEM((size, size), jnp.bfloat16)] * 3,
            pltpu.VMEM((parts, occ, rows, SEND_COLUMNS), jnp.bfloat16),
            *[dma((members, occ))] * 5,
            *[dma((2, parts))] * 3,
            dma((2,)),
            dma((parts,)),
            dma,
        ],
        compiler_params=pltpu.CompilerParams(
            collective_id=0, has_side_effects=True, vmem_limit_bytes=63 * 2**20
        ),
    )(three_index, occ_energy.reshape(1, occ), virt_energy.reshape(members, 1, rows))


def local(three_index, occ_energy, virt_energy):
    occ, rows, aux = three_index.shape
    tiles = rows % 128 == 0 and aux % SUM_COLUMNS == 0 and occ % 2 == 0
    if tiles and lax.axis_size("virt") == 4:
        return fused_local(three_index, occ_energy, virt_energy)
    return plain_local(three_index, occ_energy, virt_energy)


def solution(mesh):
    placed = (P(("copies", "blk"), "virt", None), P(("copies", "blk")), P("copies"))
    return jax.shard_map(
        local,
        mesh=mesh,
        in_specs=placed,
        out_specs=P(("copies", "blk"), "virt", None),
        check_vma=False,
    )
```

```python
import functools

import jax
import jax.numpy as jnp
from jax import lax
from jax.experimental import pallas as pl
from jax.experimental.pallas import tpu as pltpu
from jax.sharding import PartitionSpec as P

MESH = pl.DeviceIdType.MESH
SEND_COLUMNS = 256
SUM_COLUMNS = 512


def shifted(shard, axis, by):
    devices = lax.axis_size(axis)
    return lax.ppermute(shard, axis, [(i, (i + by) % devices) for i in range(devices)])


def contract(left, right):
    return lax.dot_general(
        left, right, (((1,), (1,)), ((), ())), preferred_element_type=jnp.float32
    )


def plain_local(three_index, occ_energy, virt_energy):
    occ, rows, aux = three_index.shape
    virt = virt_energy.shape[0]
    energy_rows = lax.dynamic_slice_in_dim(virt_energy, lax.axis_index("virt") * rows, rows, 0)
    part_rows = shifted(three_index, "blk", 1)
    own_full = lax.all_gather(three_index, "virt", axis=1, tiled=True)
    part_full = shifted(own_full, "blk", 1)
    energy_part = shifted(occ_energy, "blk", 1)

    def pairs(left, right):
        both = contract(left.reshape(occ * rows, aux), right.reshape(occ * virt, aux))
        return both.reshape(occ, rows, occ, virt)

    def denominator(left, right):
        return (
            left[:, None, None, None]
            + right[None, None, :, None]
            - energy_rows[None, :, None, None]
            - virt_energy[None, None, None, :]
        )

    def spread(tbar, full):
        return jnp.dot(
            tbar.astype(jnp.bfloat16).reshape(occ * rows, occ * virt),
            full.reshape(occ * virt, aux),
            preferred_element_type=jnp.float32,
        ).reshape(occ, rows, aux)

    diag = pairs(three_index, own_full)
    first = pairs(three_index, part_full)
    second = pairs(part_rows, own_full)
    own = spread(
        (2.0 * diag - diag.transpose(2, 1, 0, 3)) / denominator(occ_energy, occ_energy), own_full
    )
    own += spread(
        (2.0 * first - second.transpose(2, 1, 0, 3)) / denominator(occ_energy, energy_part),
        part_full,
    )
    partner = spread(
        (2.0 * second - first.transpose(2, 1, 0, 3)) / denominator(energy_part, occ_energy),
        own_full,
    ).astype(jnp.bfloat16)
    partner = shifted(partner, "blk", -1)
    return (own + partner.astype(jnp.float32)).astype(jnp.bfloat16)


def kernel(
    blocks,
    a_ref,
    e_ref,
    row_ref,
    o_ref,
    own_full,
    part_full,
    e_part,
    column_ref,
    acc,
    pacc,
    racc,
    psend,
    precv,
    hsend,
    hrecv,
    rsend,
    rrecv,
    k_ref,
    x_ref,
    td_ref,
    tu_ref,
    t_ref,
    staged,
    send_in,
    send_out,
    send_next,
    send_part,
    recv_own,
    recv_part,
    back_sems,
    help_sems,
    result_sems,
    e_sems,
    out_sems,
    local_sem,
):
    occ, rows, aux = a_ref.shape
    size = occ * rows
    cuts = 2 * occ
    ahead = 3
    chunks = range(aux // SEND_COLUMNS)
    v = lax.axis_index("virt")
    g = lax.axis_index("blk")
    after = lax.rem(g + 1, blocks)
    before = lax.rem(g + blocks - 1, blocks)
    step = jnp.where(v < 2, 1, -1)
    middle = (v == 1) | (v == 2)
    even = lax.rem(g, 2) == 0
    end = (v == 0) | (v == 3)
    inner = v + step
    outer = lax.rem(v - step + 4, 4)
    far = lax.rem(v + 2 * step + 4, 4)
    near = jnp.where(middle, outer, inner)
    last = jnp.where(middle, inner, far)

    def remote(src, dst, send, recv, **where):
        return pltpu.make_async_remote_copy(
            src_ref=src, dst_ref=dst, send_sem=send, recv_sem=recv,
            device_id=where, device_id_type=MESH,
        )

    def piece(ref, *lead):
        *lead, c = lead
        cols = slice((c % 2) * (aux // 2), (c % 2 + 1) * (aux // 2))
        return ref.at[(*lead, c // 2, slice(None), cols)]

    def to_inner(s, c):
        return remote(
            piece(own_full, s, c), piece(own_full, s, c), send_in.at[s, c], recv_own.at[s, c], virt=inner
        )

    def to_outer(s, c):
        return remote(
            piece(own_full, s, c), piece(own_full, s, c), send_out.at[s, c], recv_own.at[s, c], virt=outer
        )

    def to_next(s, c):
        return remote(
            piece(own_full, s, c), piece(part_full, s, c), send_next.at[s, c], recv_part.at[s, c],
            blk=after,
        )

    def part_to_inner(c):
        return remote(
            piece(part_full, v, c), piece(part_full, v, c), send_part.at[c], recv_part.at[v, c],
            virt=inner,
        )

    def back(k):
        return remote(
            psend.at[k], precv.at[k], back_sems.at[0, k], back_sems.at[1, k], blk=before
        )

    def help_back(k):
        return remote(
            hsend.at[k], hrecv.at[k], help_sems.at[0, k], help_sems.at[1, k], blk=before
        )

    def result(k):
        return remote(
            rsend.at[k], rrecv.at[k], result_sems.at[0, k], result_sems.at[1, k], virt=outer
        )

    def own_copy(make, send, c):
        return remote(
            piece(a_ref, c), piece(make, v, c), send.at[v, c],
            (recv_part if make is part_full else recv_own).at[v, c],
            **({"blk": after} if make is part_full else {"virt": inner if send is send_in else outer}),
        )

    def write(k):
        cols = slice(k * SEND_COLUMNS, (k + 1) * SEND_COLUMNS)
        return pltpu.make_async_copy(staged.at[k], o_ref.at[:, :, cols], out_sems.at[k])

    energy_copy = remote(e_ref, e_part, e_sems.at[0], e_sems.at[1], blk=after)
    keep = pltpu.make_async_copy(a_ref, own_full.at[v], local_sem)

    barrier = pltpu.get_barrier_semaphore()
    pl.semaphore_signal(barrier, inc=1, device_id={"blk": after}, device_id_type=MESH)
    pl.semaphore_signal(barrier, inc=1, device_id={"blk": before}, device_id_type=MESH)
    pl.semaphore_signal(barrier, inc=1, device_id={"virt": inner}, device_id_type=MESH)

    @pl.when(middle)
    def _():
        pl.semaphore_signal(barrier, inc=1, device_id={"virt": outer}, device_id_type=MESH)

    pl.semaphore_wait(barrier, 3 + middle.astype(jnp.int32))

    for c in range(ahead):
        own_copy(own_full, send_in, c).start()
    for c in range(ahead, cuts):
        @pl.when(end)
        def _():
            own_copy(own_full, send_in, c).start()
    for c in range(cuts):
        @pl.when(middle)
        def _():
            own_copy(own_full, send_out, c).start()
    energy_copy.start()
    for c in range(cuts):
        own_copy(part_full, send_next, c).start()
    keep.start()
    for s in range(4):
        column_ref[s] = jnp.transpose(jnp.broadcast_to(row_ref[s], (rows, rows)))[:, 0:1]
    keep.wait()

    def inverse(left, i, right, j, r, s):
        return 1.0 / (
            (left[0:1, i : i + 1] + right[0:1, j : j + 1]) - column_ref[r] - row_ref[s]
        )

    def at(i):
        return slice(i * rows, (i + 1) * rows)

    def product(left, source, s, cols, width):
        return jnp.dot(
            left[...], source[s, :, :, cols].reshape(size, width),
            preferred_element_type=jnp.float32,
        )

    def add_columns(total, left, source, s, first):
        @pl.loop(0, aux // SUM_COLUMNS)
        def _(k):
            cols = pl.ds(pl.multiple_of(k * SUM_COLUMNS, SUM_COLUMNS), SUM_COLUMNS)
            value = product(left, source, s, cols, SUM_COLUMNS)
            if first:
                total[:, cols] = value
            else:
                total[:, cols] += value

    def shard(source, s):
        return source[s].reshape(size, aux)

    def part_arrives(s):
        for c in range(cuts):
            to_next(s, c).wait_recv()

    def pair_ratio(r, s, ratio_ref):
        k_ref[...] = contract(shard(own_full, r), shard(own_full, s))
        for i in range(occ):
            for j in range(occ):
                ratio_ref[at(i), at(j)] = (
                    (2.0 * k_ref[at(i), at(j)] - k_ref[at(j), at(i)])
                    * inverse(e_ref, i, e_ref, j, r, s)
                ).astype(jnp.bfloat16)

    def diagonal(r, s, total, first):
        pair_ratio(r, s, tu_ref)
        add_columns(total, tu_ref, own_full, s, first)

    def cross(r, s, wait):
        k_ref[...] = contract(shard(part_full, r), shard(own_full, s))
        if wait:
            part_arrives(s)
        x_ref[...] = contract(shard(own_full, r), shard(part_full, s))
        amplitudes(r, s)

    def amplitudes(r, s):
        for i in range(occ):
            for j in range(occ):
                scale = inverse(e_ref, i, e_part, j, r, s)
                x = x_ref[at(i), at(j)]
                y = k_ref[at(j), at(i)]
                t_ref[at(i), at(j)] = ((2.0 * x - y) * scale).astype(jnp.bfloat16)
                tu_ref[at(j), at(i)] = ((2.0 * y - x) * scale).astype(jnp.bfloat16)

    def spread(s, first):
        add_columns(pacc, tu_ref, own_full, s, first)
        add_columns(acc, t_ref, part_full, s, False)

    def from_outer(c):
        to_outer(outer, c).wait_recv()
        to_inner(outer, c).start()

        @pl.when(even)
        def _():
            to_next(outer, c).start()

    def from_partner(c):
        to_inner(inner, c).wait_recv()
        to_outer(inner, c).start()
        to_next(inner, c).start()

    def from_far(c):
        to_inner(far, c).wait_recv()
        to_next(far, c).start()

    def from_inner(s, c):
        to_inner(s, c).wait_recv()
        to_next(s, c).start()

    diagonal(v, v, acc, True)
    energy_copy.wait_recv()

    for c in range(occ):
        @pl.when(middle)
        def _():
            from_outer(c)
            if c < ahead:
                from_partner(c)

        @pl.when(end)
        def _():
            from_inner(inner, c)

    part_arrives(v)

    @pl.when(end & even)
    def _():
        for c in range(cuts):
            part_to_inner(c).start()

    cross(v, v, False)
    spread(v, True)

    for c in range(occ, cuts):
        @pl.when(middle)
        def _():
            from_outer(c)

        @pl.when(end)
        def _():
            from_inner(inner, c)

    @pl.when(middle)
    def _():
        for c in range(ahead, cuts):
            own_copy(own_full, send_in, c).start()
        for c in range(occ):
            from_far(c)

    diagonal(v, near, acc, False)

    @pl.when(middle)
    def _():
        for c in range(occ, cuts - 1):
            from_far(c)

    @pl.when(end)
    def _():
        cross(v, near, True)
        spread(near, False)

    @pl.when(middle)
    def _():
        from_far(cuts - 1)
        pair_ratio(outer, far, td_ref)
        from_partner(ahead)
        part_arrives(outer)
        cross(outer, far, True)
        from_partner(ahead + 1)
        for k in chunks:
            cols = slice(k * SEND_COLUMNS, (k + 1) * SEND_COLUMNS)
            hsend[k] = product(tu_ref, own_full, far, cols, SEND_COLUMNS).astype(jnp.bfloat16)
            help_back(k).start()
        from_partner(ahead + 2)

        @pl.loop(0, aux // SUM_COLUMNS)
        def _(k):
            cols = pl.ds(pl.multiple_of(k * SUM_COLUMNS, SUM_COLUMNS), SUM_COLUMNS)
            racc[:, cols] = product(td_ref, own_full, far, cols, SUM_COLUMNS) + product(
                t_ref, part_full, far, cols, SUM_COLUMNS
            )

        for c in range(ahead + 3, cuts - 1):
            from_partner(c)
        diagonal(v, far, acc, False)
        from_partner(cuts - 1)
        for k in chunks:
            cols = slice(k * SEND_COLUMNS, (k + 1) * SEND_COLUMNS)
            help_back(k).wait_recv()
            rsend[k] = (racc[:, cols] + hrecv[k].astype(jnp.float32)).astype(jnp.bfloat16)
            result(k).start()
        cross(v, outer, False)
        spread(outer, False)
        cross(v, far, False)
        spread(far, False)

    @pl.when(end)
    def _():
        for c in range(cuts):
            from_inner(far, c)

    diagonal(v, last, acc, False)
    cross(v, last, True)
    for k in chunks:
        cols = slice(k * SEND_COLUMNS, (k + 1) * SEND_COLUMNS)
        psend[k] = (
            pacc[:, cols] + product(tu_ref, own_full, last, cols, SEND_COLUMNS)
        ).astype(jnp.bfloat16)
        back(k).start()
    add_columns(acc, t_ref, part_full, last, False)
    for k in chunks:
        cols = slice(k * SEND_COLUMNS, (k + 1) * SEND_COLUMNS)

        @pl.when(end)
        def _():
            result(k).wait_recv()
            acc[:, cols] += rrecv[k].astype(jnp.float32)

        back(k).wait_recv()
        staged[k] = (
            (acc[:, cols] + precv[k].astype(jnp.float32))
            .astype(jnp.bfloat16)
            .reshape(occ, rows, SEND_COLUMNS)
        )
        write(k).start()

    energy_copy.wait_send()
    for k in chunks:
        back(k).wait_send()
        write(k).wait()
    for c in range(cuts):
        for s in (v, inner, far):
            to_next(s, c).wait_send()
        to_inner(v, c).wait_send()

        @pl.when(middle)
        def _():
            to_inner(outer, c).wait_send()
            to_outer(v, c).wait_send()
            to_outer(inner, c).wait_send()

        @pl.when(middle & even)
        def _():
            to_next(outer, c).wait_send()

        @pl.when(end & even)
        def _():
            part_to_inner(c).wait_send()

    @pl.when(middle)
    def _():
        for k in chunks:
            help_back(k).wait_send()
            result(k).wait_send()


def fused_local(three_index, occ_energy, virt_energy):
    occ, rows, aux = three_index.shape
    members, blocks = lax.axis_size("virt"), lax.axis_size("blk")
    size, parts = occ * rows, aux // SEND_COLUMNS
    vmem = pl.BlockSpec(memory_space=pltpu.VMEM)
    dma = pltpu.SemaphoreType.DMA
    full = pltpu.VMEM((members, occ, rows, aux), jnp.bfloat16)
    total = pltpu.VMEM((size, aux), jnp.float32)
    pieces = pltpu.VMEM((parts, size, SEND_COLUMNS), jnp.bfloat16)
    return pl.pallas_call(
        functools.partial(kernel, blocks),
        out_shape=jax.ShapeDtypeStruct((occ, rows, aux), jnp.bfloat16),
        in_specs=[pl.BlockSpec(memory_space=pl.ANY), vmem, vmem],
        out_specs=pl.BlockSpec(memory_space=pl.ANY),
        scratch_shapes=[
            full,
            full,
            pltpu.VMEM((1, occ), jnp.float32),
            pltpu.VMEM((members, rows, 1), jnp.float32),
            *[total] * 3,
            *[pieces] * 6,
            *[pltpu.VMEM((size, size), jnp.float32)] * 2,
            *[pltpu.VMEM((size, size), jnp.bfloat16)] * 3,
            pltpu.VMEM((parts, occ, rows, SEND_COLUMNS), jnp.bfloat16),
            *[dma((members, 2 * occ))] * 3,
            dma((2 * occ,)),
            *[dma((members, 2 * occ))] * 2,
            *[dma((2, parts))] * 3,
            dma((2,)),
            dma((parts,)),
            dma,
        ],
        compiler_params=pltpu.CompilerParams(
            collective_id=0, has_side_effects=True, vmem_limit_bytes=63 * 2**20
        ),
    )(three_index, occ_energy.reshape(1, occ), virt_energy.reshape(members, 1, rows))


def local(three_index, occ_energy, virt_energy):
    occ, rows, aux = three_index.shape
    tiles = rows % 128 == 0 and aux % SUM_COLUMNS == 0 and occ >= 4
    if tiles and lax.axis_size("virt") == 4 and lax.axis_size("blk") % 2 == 0:
        return fused_local(three_index, occ_energy, virt_energy)
    return plain_local(three_index, occ_energy, virt_energy)


def solution(mesh):
    placed = (P(("copies", "blk"), "virt", None), P(("copies", "blk")), P("copies"))
    return jax.shard_map(
        local,
        mesh=mesh,
        in_specs=placed,
        out_specs=P(("copies", "blk"), "virt", None),
        check_vma=False,
    )
```
